32 devices in a mesh: dp: 4 (over x, core), cls: 8 (over z, y).
Axes of the slice: x: 2, y: 2, z: 4, core: 2. Of those that a mesh axis runs over, the one named last changes fastest.
Arguments:
- pooled: bfloat16 [4096, 512], P(('dp', 'cls')), may hold values from -6 to 6
- proj: bfloat16 [512, 512], replicated, may hold values from -0.25 to 0.25
- centers: bfloat16 [2048, 512], P('cls'), may hold values from -6 to 6
- labels: int32 [4096], P(('dp', 'cls')), may hold values from 0 to 2047
- row_weight: bfloat16 [4096], P(('dp', 'cls')), may hold values from 0.5 to 2
Outputs:
- row_loss: float32 [4096], P(('dp', 'cls'))
- center_grad: float32 [2048, 512], P('cls')
- proj_grad: float32 [512, 512], replicated
The draws below stay inside these ranges and needn't reach their ends.
All inputs are finite; a program needn't handle non-finite values.
Results may differ from the reference program's by a relative error of at most 0.005.
Values may be sent and summed in bfloat16 or wider, within the bound.
No kernel may reach another device: no remote copies, remote signals or barrier semaphores. Data moves between devices by JAX's collectives and lax.ppermute only.
A program may use at most 128 MiB of HBM per device.

```python
import math
import jax
import jax.numpy as jnp
import numpy as np
from jax import lax

D = 512
FEAT = 512
BATCH = 4096
CLASSES = 2048


def plant(drawn, rng, least, largest):
    index_at = [jax.random.randint(jax.random.fold_in(rng, axis), (), 0, length) for axis, length in enumerate(drawn.shape)]
    main_axis = drawn.shape.index(max(drawn.shape))
    next_to = index_at[:main_axis] + [(index_at[main_axis] + 1) % drawn.shape[main_axis]] + index_at[main_axis + 1:]
    return drawn.at[tuple(index_at)].set(least).at[tuple(next_to)].set(largest)


def level_of(own_key, extent, split, low, largest):
    factor_of, own = 1.0, jax.random.fold_in(own_key, 6)
    for position, parts in split:
        heights = jnp.exp(jax.random.uniform(jax.random.fold_in(own, position), (parts,), jnp.float32, low / len(split), largest / len(split)))
        factor_of = factor_of * jnp.repeat(heights, extent[position] // parts).reshape([-1 if axis == position else 1 for axis in range(len(extent))])
    return factor_of


def cumulative_ranks(amount, skew):
    weights = [(1 << 20) // math.isqrt(rank ** skew) + 1 for rank in range(1, amount + 1)]
    scale = 1 + sum(weights) // (1 << 30)
    return np.cumsum(np.array([max(1, weight // scale) for weight in weights]))


def skewed_ids(stream_key, shape, count, lean):
    listing = cumulative_ranks(count, lean)
    lot = jax.random.randint(jax.random.fold_in(stream_key, 1), shape, 0, int(listing[count - 1]))
    grade = jnp.searchsorted(jnp.asarray(listing, jnp.int32), lot, side="right")
    return jax.random.permutation(jax.random.fold_in(stream_key, 2), count)[grade].astype(jnp.int32)


def scatter_about(own_key, extent, deviation, most, cuts=(), kind=jnp.bfloat16):
    values = deviation * jax.random.normal(own_key, extent, jnp.float32)
    if cuts:
        values = values * level_of(own_key, extent, cuts, -0.22, 0.18)
    return jnp.clip(values, -most, most).astype(kind)


def setup_inputs(seed: int = 0) -> dict:
    streams_of = jax.random.split(jax.random.key(seed), 6)
    pooled = scatter_about(streams_of[0], (BATCH, FEAT), 1.0, 6.0, ((0, 32),))
    proj = scatter_about(streams_of[1], (FEAT, D), FEAT ** -0.5, 0.25)
    centers = scatter_about(streams_of[2], (CLASSES, D), 1.0, 6.0, ((0, 8),))
    labels = plant(skewed_ids(streams_of[3], (BATCH,), CLASSES, 2), jax.random.fold_in(streams_of[3], 3), 0, CLASSES - 1).astype(jnp.int32)
    row_weight = jnp.clip(jnp.exp(math.log(2.0) - 1.3862944 * jax.random.uniform(streams_of[4], (BATCH,), jnp.float32) ** level_of(streams_of[4], (BATCH,), ((0, 32),), -0.2, 0.2)), 0.5, 2.0).astype(jnp.bfloat16)
    return {"pooled": pooled, "proj": proj, "centers": centers, "labels": labels, "row_weight": row_weight}


SCALE = 64.0
MARGIN = 0.35
EPS = 1e-06

def unit_rows(values):
    inverse = lax.rsqrt(lax.optimization_barrier(jnp.sum(values * values, axis=1, keepdims=True)) + EPS)
    return ((values * inverse).astype(jnp.bfloat16), inverse)

def reference(pooled, proj, centers, labels, row_weight):
    hidden = jnp.dot(pooled, proj, preferred_element_type=jnp.float32)
    emb, z_inv = unit_rows(hidden)
    unit, c_inv = unit_rows(centers.astype(jnp.float32))
    block = math.gcd(BATCH, 512)
    count = BATCH // block
    columns = jnp.arange(CLASSES, dtype=jnp.int32)

    def step(accum, pieces):
        emb_block, lab_block, weight_block = pieces
        cosine = lax.dot_general(emb_block, unit, (((1,), (1,)), ((), ())), preferred_element_type=jnp.float32)
        onehot = (lab_block[:, None] == columns[None, :]).astype(jnp.float32)
        logits = SCALE * cosine - SCALE * MARGIN * onehot
        expo = jnp.exp(logits)
        total = lax.optimization_barrier(jnp.sum(expo, axis=1))
        target = lax.optimization_barrier(jnp.sum(logits * onehot, axis=1))
        grad_logits = (weight_block.astype(jnp.float32)[:, None] * (expo / total[:, None] - onehot)).astype(jnp.bfloat16)
        accum = accum + SCALE * lax.dot_general(grad_logits, emb_block, (((0,), (0,)), ((), ())), preferred_element_type=jnp.float32)
        grad_emb = SCALE * jnp.dot(grad_logits, unit, preferred_element_type=jnp.float32)
        return (accum, (jnp.log(total) - target, grad_emb))
    grad_unit, (losses, grad_emb) = lax.scan(step, jnp.zeros((CLASSES, D), jnp.float32), (emb.reshape(count, block, D), labels.reshape(count, block), row_weight.reshape(count, block)))
    row_loss = losses.reshape(BATCH)
    grad_emb = grad_emb.reshape(BATCH, D)
    unit_f = unit.astype(jnp.float32)
    center_grad = c_inv * (grad_unit - unit_f * lax.optimization_barrier(jnp.sum(unit_f * grad_unit, axis=1, keepdims=True)))
    emb_f = emb.astype(jnp.float32)
    grad_hidden = z_inv * (grad_emb - emb_f * lax.optimization_barrier(jnp.sum(emb_f * grad_emb, axis=1, keepdims=True)))
    proj_grad = lax.dot_general(pooled.astype(jnp.float32), grad_hidden, (((0,), (0,)), ((), ())), precision=lax.Precision.HIGHEST, preferred_element_type=jnp.float32)
    return (row_loss, center_grad, proj_grad)
```

```python
import jax
import jax.numpy as jnp
from jax import lax
from jax.sharding import PartitionSpec as P

SCALE = 64.0
MARGIN = 0.35
EPS = 1e-06
F32 = jnp.float32
BF16 = jnp.bfloat16


def unit_rows(values):
    inverse = lax.rsqrt(jnp.sum(values * values, axis=1, keepdims=True) + EPS)
    return ((values * inverse).astype(BF16), inverse)


def swap(x, axis, mask):
    size = lax.axis_size(axis)
    return lax.ppermute(x, axis, [(i, i ^ mask) for i in range(size)])


def dot(a, b, ca, cb):
    return lax.dot_general(a, b, (((ca,), (cb,)), ((), ())), preferred_element_type=F32)


def scatter_sum(x, axis):
    size = lax.axis_size(axis)
    if size == 1:
        return x
    index = lax.axis_index(axis)
    rows = x.shape[0] // size
    total = lax.dynamic_slice_in_dim(x, index * rows, rows)
    for mask in range(1, size):
        out = lax.dynamic_slice_in_dim(x, (index ^ mask) * rows, rows).astype(BF16)
        total = total + swap(out, axis, mask).astype(F32)
    return total


def gather_rows(x, axis):
    size = lax.axis_size(axis)
    if size == 1:
        return x
    index = lax.axis_index(axis)
    parts = [x] + [swap(x, axis, mask) for mask in range(1, size)]
    if size == 2:
        low = jnp.where(index == 0, parts[0], parts[1])
        high = jnp.where(index == 0, parts[1], parts[0])
        return jnp.concatenate([low, high], axis=0)
    full = jnp.zeros((size * x.shape[0],) + x.shape[1:], x.dtype)
    for mask, part in enumerate(parts):
        full = lax.dynamic_update_slice_in_dim(full, part, (index ^ mask) * x.shape[0], 0)
    return full


def on_device(pooled, proj, centers, labels, row_weight):
    ns, nk = lax.axis_size("s"), lax.axis_size("k")
    nh, nl = lax.axis_size("dh"), lax.axis_size("dl")
    rows, width = pooled.shape
    c_dev = centers.shape[0]
    at_s, at_k = lax.axis_index("s"), lax.axis_index("k")
    meta = jnp.stack([labels.astype(F32), row_weight.astype(F32)])
    feats = jnp.concatenate([pooled] + [swap(pooled, "s", m) for m in range(1, ns)], axis=0)
    metas = jnp.concatenate([meta] + [swap(meta, "s", m) for m in range(1, ns)], axis=1)
    cents = jnp.concatenate([centers] + [swap(centers, "k", j) for j in range(1, nk)], axis=0)
    label_all = metas[0:1].astype(jnp.int32)
    weight_all = metas[1:2]
    unit, c_inv = unit_rows(cents.astype(F32))
    hidden = dot(feats, proj, 1, 0)
    emb, z_inv = unit_rows(hidden)
    local = lax.broadcasted_iota(jnp.int32, (c_dev, 1), 0)
    ids = jnp.concatenate([local + (at_s * nk + (at_k ^ j)) * c_dev for j in range(nk)], axis=0)
    onehot = (ids == label_all).astype(F32)
    logits = SCALE * dot(unit, emb, 1, 1) - SCALE * MARGIN * onehot
    expo = jnp.exp(logits)
    stats = jnp.stack([jnp.sum(expo, axis=0), jnp.sum(logits * onehot, axis=0)]).reshape(2, ns, rows)
    total = stats
    for m in range(1, ns):
        other = swap(stats, "s", m)
        total = total + jnp.stack([other[:, b ^ m] for b in range(ns)], axis=1)
    row_loss = jnp.log(total[0, 0]) - total[1, 0]
    total_all = total[0].reshape(1, ns * rows)
    grad = (weight_all * (expo / total_all - onehot)).astype(BF16)
    grad_unit = SCALE * dot(grad, emb, 1, 0)
    grad_emb = SCALE * dot(grad, unit, 0, 0)
    emb_f = emb.astype(F32)
    grad_hidden = z_inv * (grad_emb - emb_f * jnp.sum(emb_f * grad_emb, axis=1, keepdims=True))
    proj_part = dot(feats, grad_hidden.astype(BF16), 0, 0)

    cg = grad_unit[:c_dev]
    for j in range(1, nk):
        cg = cg + swap(grad_unit[j * c_dev : (j + 1) * c_dev].astype(BF16), "k", j).astype(F32)
    half = scatter_sum(cg, "dl").astype(BF16)
    summed = half.astype(F32)
    for m in range(1, nh):
        summed = summed + swap(half, "dh", m).astype(F32)
    at_l = lax.axis_index("dl")
    part = c_dev // nl
    unit_f = lax.dynamic_slice_in_dim(unit[:c_dev], at_l * part, part).astype(F32)
    inv = lax.dynamic_slice_in_dim(c_inv[:c_dev], at_l * part, part)
    center_half = inv * (summed - unit_f * jnp.sum(unit_f * summed, axis=1, keepdims=True))
    center_grad = gather_rows(center_half, "dl")

    rest = ("dh", "s", "k")
    n_rest = nh * ns * nk
    quarter = scatter_sum(proj_part, "dl").astype(BF16)
    pieces = lax.all_to_all(quarter.reshape(n_rest, -1, width), rest, 0, 0)
    piece = jnp.sum(pieces.astype(F32), axis=0, keepdims=True).astype(BF16)
    back = lax.all_to_all(jnp.broadcast_to(piece, pieces.shape), rest, 0, 0)
    proj_grad = gather_rows(back.reshape(quarter.shape), "dl").astype(F32)
    return (row_loss, center_grad, proj_grad)


def solution(mesh):
    dp, cls = mesh.shape["dp"], mesh.shape["cls"]
    nl = 2 if dp % 2 == 0 else 1
    bits = cls.bit_length() - 1
    ns = 1 << ((bits + 1) // 2)
    fine = jax.sharding.Mesh(
        mesh.devices.reshape(dp // nl, nl, ns, cls // ns), ("dh", "dl", "s", "k")
    )
    dp_axes, cls_axes = ("dh", "dl"), ("s", "k")
    every = dp_axes + cls_axes
    in_specs = (P(every, None), P(), P(cls_axes, None), P(every), P(every))
    out_specs = (P(every), P(cls_axes, None), P())
    return jax.shard_map(
        on_device, mesh=fine, in_specs=in_specs, out_specs=out_specs, check_vma=False
    )
```

```python
import math

import jax
import jax.numpy as jnp
from jax import lax
from jax.sharding import PartitionSpec as P

SCALE = 64.0
MARGIN = 0.35
EPS = 1e-06
DIGIT = 128
F32 = jnp.float32
BF16 = jnp.bfloat16


def unit_rows(values):
    inverse = lax.rsqrt(jnp.sum(values * values, axis=1, keepdims=True) + EPS)
    return ((values * inverse).astype(BF16), inverse)


def size_of(axes):
    return math.prod(lax.axis_size(a) for a in axes)


def swap(x, axes, mask):
    return lax.ppermute(x, axes, [(i, i ^ mask) for i in range(size_of(axes))])


def dot(a, b, ca, cb):
    return lax.dot_general(a, b, (((ca,), (cb,)), ((), ())), preferred_element_type=F32)


def scatter_sum(x, axes):
    size = size_of(axes)
    if size == 1:
        return x
    index = lax.axis_index(axes)
    rows = x.shape[0] // size
    total = lax.dynamic_slice_in_dim(x, index * rows, rows)
    for mask in range(1, size):
        out = lax.dynamic_slice_in_dim(x, (index ^ mask) * rows, rows).astype(BF16)
        total = total + swap(out, axes, mask).astype(F32)
    return total


def full_sum(x, axes):
    groups = [axes] if size_of(axes) <= 4 else [(a,) for a in axes]
    for group in groups:
        size = size_of(group)
        sent = x.astype(BF16)
        parts = [sent] + [swap(sent, group, mask) for mask in range(1, size)]
        span = size
        while span > 1:
            parts = [parts[i].astype(F32) + parts[i + span // 2].astype(F32) for i in range(span // 2)]
            span //= 2
        x = parts[0]
    return x


def gather_rows(x, axes):
    size = size_of(axes)
    if size == 1:
        return x
    index = lax.axis_index(axes)
    full = jnp.zeros((size * x.shape[0],) + x.shape[1:], x.dtype)
    full = lax.dynamic_update_slice_in_dim(full, x, index * x.shape[0], 0)
    for mask in range(1, size):
        part = swap(x, axes, mask)
        full = lax.dynamic_update_slice_in_dim(full, part, (index ^ mask) * x.shape[0], 0)
    return full


def on_device(pooled, proj, centers, labels, row_weight):
    s_axes = ("sz", "sy")
    ns, nk, nl = size_of(s_axes), size_of(("k",)), size_of(("dl",))
    rows, width = pooled.shape
    c_dev = centers.shape[0]
    half = c_dev // nl
    at_s, at_k, at_l = (lax.axis_index(a) for a in (s_axes, "k", "dl"))
    meta = jnp.concatenate([(labels // DIGIT).astype(BF16), (labels % DIGIT).astype(BF16), row_weight])
    meta_rows = -(-3 * rows // width)
    pad = (-meta_rows) % 8
    meta = jnp.pad(meta, (0, (meta_rows + pad) * width - 3 * rows)).reshape(-1, width)
    packed = jnp.concatenate([pooled, meta], axis=0)
    blocks = [packed] + [swap(packed, s_axes, m) for m in range(1, ns)]
    feats = jnp.concatenate([b[:rows] for b in blocks], axis=0)
    metas = [b[rows:].reshape(1, -1) for b in blocks]
    high, low, weight_all = (
        jnp.concatenate([m[:, i * rows : (i + 1) * rows] for m in metas], axis=1).astype(F32) for i in range(3)
    )
    label_all = (high * DIGIT + low).astype(jnp.int32)
    mine = [lax.dynamic_slice_in_dim(centers, (at_l ^ c) * half, half) for c in range(nl)]
    cents = list(mine)
    for j in range(1, nk):
        got = swap(mine[0], ("k",), j)
        cents += [got] + [swap(got, ("dl",), c) for c in range(1, nl)]
    unit, c_inv = unit_rows(jnp.concatenate(cents, axis=0).astype(F32))
    hidden = dot(feats, proj, 1, 0)
    emb, z_inv = unit_rows(hidden)
    local = lax.broadcasted_iota(jnp.int32, (half, 1), 0)
    ids = jnp.concatenate(
        [local + ((at_k ^ j) * ns + at_s) * c_dev + (at_l ^ c) * half for j in range(nk) for c in range(nl)], axis=0
    )
    onehot = (ids == label_all).astype(F32)
    logits = SCALE * dot(unit, emb, 1, 1) - SCALE * MARGIN * onehot
    expo = jnp.exp(logits)
    stats = jnp.stack([jnp.sum(expo, axis=0), jnp.sum(logits * onehot, axis=0)])
    total = stats
    for m in range(1, ns):
        other = swap(stats, s_axes, m)
        total = total + jnp.concatenate([other[:, (b ^ m) * rows : ((b ^ m) + 1) * rows] for b in range(ns)], axis=1)
    row_loss = jnp.log(total[0, :rows]) - total[1, :rows]
    grad = (weight_all * (expo / total[0:1] - onehot)).astype(BF16)
    grad_emb = SCALE * dot(grad, unit, 0, 0)
    emb_f = emb.astype(F32)
    grad_hidden = z_inv * (grad_emb - emb_f * jnp.sum(emb_f * grad_emb, axis=1, keepdims=True))
    proj_part = dot(feats, grad_hidden.astype(BF16), 0, 0)
    grad_unit = SCALE * dot(grad, emb, 1, 0)

    first, second = ("dh", "sy"), ("k", "sz")
    piece = scatter_sum(scatter_sum(proj_part, ("dl",)), first)
    piece = full_sum(piece, second).astype(BF16)
    proj_grad = gather_rows(gather_rows(piece, first), ("dl",)).astype(F32)

    cg = grad_unit.reshape(nk, nl, half, width)
    own = cg[:, 0]
    for c in range(1, nl):
        own = own + swap(cg[:, c].astype(BF16), ("dl",), c).astype(F32)
    summed = own[0]
    for j in range(1, nk):
        summed = summed + swap(own[j].astype(BF16), ("k",), j).astype(F32)
    summed = full_sum(summed, ("dh",))
    unit_f = unit[:half].astype(F32)
    center_part = c_inv[:half] * (summed - unit_f * jnp.sum(unit_f * summed, axis=1, keepdims=True))
    center_grad = gather_rows(center_part, ("dl",))
    return (row_loss, center_grad, proj_grad)


def solution(mesh):
    dp, cls = mesh.shape["dp"], mesh.shape["cls"]
    nl = 2 if dp % 2 == 0 else 1
    bits = cls.bit_length() - 1
    ns = 1 << ((bits + 1) // 2)
    sy = min(2, ns)
    fine = jax.sharding.Mesh(
        mesh.devices.reshape(dp // nl, nl, cls // ns, ns // sy, sy), ("dh", "dl", "k", "sz", "sy")
    )
    dp_axes, cls_axes = ("dh", "dl"), ("k", "sz", "sy")
    every = dp_axes + cls_axes
    in_specs = (P(every, None), P(), P(cls_axes, None), P(every), P(every))
    out_specs = (P(every), P(cls_axes, None), P())
    return jax.shard_map(
        on_device, mesh=fine, in_specs=in_specs, out_specs=out_specs, check_vma=False
    )
```

```python
import math

import jax
import jax.numpy as jnp
from jax import lax
from jax.sharding import PartitionSpec as P


SCALE = 64.0
MARGIN = 0.35
EPS = 1e-06
F32 = jnp.float32
BF16 = jnp.bfloat16


def unit_rows(values):
    inverse = lax.rsqrt(jnp.sum(values * values, axis=1, keepdims=True) + EPS)
    return ((values * inverse).astype(BF16), inverse)


def size_of(axes):
    return math.prod(lax.axis_size(a) for a in axes)


def swap(x, axes, mask):
    return lax.ppermute(x, axes, [(i, i ^ mask) for i in range(size_of(axes))])


def dot(a, b, ca, cb):
    return lax.dot_general(a, b, (((ca,), (cb,)), ((), ())), preferred_element_type=F32)


def scatter_sum(x, axes):
    size = size_of(axes)
    if size == 1:
        return x
    index = lax.axis_index(axes)
    rows = x.shape[0] // size
    total = lax.dynamic_slice_in_dim(x, index * rows, rows)
    sent = [lax.dynamic_slice_in_dim(x, (index ^ mask) * rows, rows).astype(BF16) for mask in range(1, size)]
    parts = [swap(out, axes, mask) for mask, out in enumerate(sent, 1)]
    for part in parts:
        total = total + part.astype(F32)
    return total


def full_sum(x, axes):
    groups = [axes] if size_of(axes) <= 4 else [(a,) for a in axes]
    for group in groups:
        size = size_of(group)
        sent = x.astype(BF16)
        parts = [sent] + [swap(sent, group, mask) for mask in range(1, size)]
        span = size
        while span > 1:
            parts = [parts[i].astype(F32) + parts[i + span // 2].astype(F32) for i in range(span // 2)]
            span //= 2
        x = parts[0]
    return x


def gather_rows(x, axes):
    size = size_of(axes)
    if size == 1:
        return x
    index = lax.axis_index(axes)
    full = jnp.zeros((size * x.shape[0],) + x.shape[1:], x.dtype)
    full = lax.dynamic_update_slice_in_dim(full, x, index * x.shape[0], 0)
    for mask in range(1, size):
        part = swap(x, axes, mask)
        full = lax.dynamic_update_slice_in_dim(full, part, (index ^ mask) * x.shape[0], 0)
    return full


def on_device(pooled, proj, centers, labels, row_weight):
    s_axes = ("sz", "sy")
    ns, nk, nl = size_of(s_axes), size_of(("k",)), size_of(("dl",))
    rows, _ = pooled.shape
    c_dev = centers.shape[0]
    half = c_dev // nl
    at_s, at_k, at_l = (lax.axis_index(a) for a in (s_axes, "k", "dl"))
    mine = lax.optimization_barrier(lax.dynamic_slice_in_dim(centers, at_l * half, half))
    own_parts = [mine] + [swap(mine, ("k",), j) for j in range(1, nk)]
    blocks = [pooled] + [swap(pooled, s_axes, m) for m in range(1, ns)]
    meta = lax.optimization_barrier(jnp.concatenate([labels.astype(F32), row_weight.astype(F32)]).reshape(1, 2 * rows))
    metas = [meta] + [swap(meta, s_axes, m) for m in range(1, ns)]
    label_of = [m[:, :rows].astype(jnp.int32) for m in metas]
    weights = [m[:, rows:] for m in metas]
    cents = list(own_parts)
    for c in range(1, nl):
        cents.append(lax.dynamic_slice_in_dim(centers, (at_l ^ c) * half, half))
        cents += [swap(own_parts[j], ("dl",), c) for j in range(1, nk)]
    pairs = [unit_rows(part.astype(F32)) for part in cents]
    unit = jnp.concatenate([p[0] for p in pairs], axis=0)
    c_inv = pairs[0][1]
    label_all = jnp.concatenate(label_of, axis=1)
    weight_all = jnp.concatenate(weights, axis=1)
    local = lax.broadcasted_iota(jnp.int32, (half, 1), 0)
    ids = jnp.concatenate(
        [local + ((at_k ^ j) * ns + at_s) * c_dev + (at_l ^ c) * half for c in range(nl) for j in range(nk)], axis=0
    )
    embs, z_invs, expos, stats = [], [], [], []
    for m in range(ns):
        emb, z_inv = unit_rows(dot(blocks[m], proj, 1, 0))
        onehot = (ids == label_of[m]).astype(F32)
        logits = SCALE * dot(unit, emb, 1, 1) - SCALE * MARGIN * onehot
        expo = jnp.exp(logits)
        stats.append((jnp.sum(expo, axis=0, keepdims=True), jnp.sum(logits * onehot, axis=0, keepdims=True)))
        embs.append(emb)
        z_invs.append(z_inv)
        expos.append(expo)
    stats = jnp.concatenate([s[0] for s in stats] + [s[1] for s in stats], axis=1)
    total, target = stats[:, : ns * rows], stats[:, ns * rows : ns * rows + rows]
    for m in range(1, ns):
        other = swap(stats, s_axes, m)
        total = total + jnp.concatenate([other[:, (b ^ m) * rows : ((b ^ m) + 1) * rows] for b in range(ns)], axis=1)
        target = target + other[:, (ns + m) * rows : (ns + m + 1) * rows]
    row_loss = (jnp.log(total[:, :rows]) - target).reshape(rows)
    feats, emb, z_inv = (jnp.concatenate(x, axis=0) for x in (blocks, embs, z_invs))
    expo = jnp.concatenate(expos, axis=1)
    onehot = (ids == label_all).astype(F32)
    grad = (weight_all * (expo / total - onehot)).astype(BF16)
    grad_emb = SCALE * dot(grad, unit, 0, 0)
    emb_f = emb.astype(F32)
    grad_hidden = (z_inv * (grad_emb - emb_f * jnp.sum(emb_f * grad_emb, axis=1, keepdims=True))).astype(BF16)

    span = nk * half
    own = SCALE * dot(grad[:span], emb, 1, 0)
    for c in range(1, nl):
        send = (SCALE * dot(grad[c * span : (c + 1) * span], emb, 1, 0)).astype(BF16)
        own = own + swap(send, ("dl",), c).astype(F32)
    summed = own[:half]
    for j in range(1, nk):
        summed = summed + swap(own[j * half : (j + 1) * half].astype(BF16), ("k",), j).astype(F32)
    summed = full_sum(summed, ("dh",))
    unit_f = unit[:half].astype(F32)
    center_part = c_inv * (summed - unit_f * jnp.sum(unit_f * summed, axis=1, keepdims=True))
    center_grad = gather_rows(center_part, ("dl",))
    first, second = ("dh", "sy"), ("k", "sz")
    cols = feats.shape[1] // nl
    sends = [dot(lax.dynamic_slice_in_dim(feats, (at_l ^ c) * cols, cols, 1), grad_hidden, 0, 0).astype(BF16) for c in range(1, nl)]
    piece = dot(lax.dynamic_slice_in_dim(feats, at_l * cols, cols, 1), grad_hidden, 0, 0)
    piece = lax.optimization_barrier(piece)
    for c in range(1, nl):
        piece = piece + swap(sends[c - 1], ("dl",), c).astype(F32)
    piece = scatter_sum(piece, first)
    piece = full_sum(piece, second)
    piece = piece.astype(BF16)
    proj_grad = gather_rows(gather_rows(piece, first), ("dl",)).astype(F32)

    return (row_loss, center_grad, proj_grad)


def solution(mesh):
    dp, cls = mesh.shape["dp"], mesh.shape["cls"]
    nl = 2 if dp % 2 == 0 else 1
    bits = cls.bit_length() - 1
    ns = 1 << ((bits + 1) // 2)
    sy = min(2, ns)
    fine = jax.sharding.Mesh(
        mesh.devices.reshape(dp // nl, nl, cls // ns, ns // sy, sy), ("dh", "dl", "k", "sz", "sy")
    )
    dp_axes, cls_axes = ("dh", "dl"), ("k", "sz", "sy")
    every = dp_axes + cls_axes
    in_specs = (P(every, None), P(), P(cls_axes, None), P(every), P(every))
    out_specs = (P(every), P(cls_axes, None), P())

    return jax.shard_map(on_device, mesh=fine, in_specs=in_specs, out_specs=out_specs, check_vma=False)
```

```python
import math

import jax
import jax.numpy as jnp
from jax import lax
from jax.sharding import PartitionSpec as P


SCALE = 64.0
MARGIN = 0.35
EPS = 1e-06
F32 = jnp.float32
BF16 = jnp.bfloat16


def unit_rows(values):
    inverse = lax.rsqrt(jnp.sum(values * values, axis=1, keepdims=True) + EPS)
    return ((values * inverse).astype(BF16), inverse)


def size_of(axes):
    return math.prod(lax.axis_size(a) for a in axes)


def swap(x, axes, mask):
    return lax.ppermute(x, axes, [(i, i ^ mask) for i in range(size_of(axes))])


def dot(a, b, ca, cb):
    return lax.dot_general(a, b, (((ca,), (cb,)), ((), ())), preferred_element_type=F32)


def scatter_sum(x, axes):
    size = size_of(axes)
    if size == 1:
        return x
    index = lax.axis_index(axes)
    rows = x.shape[0] // size
    total = lax.dynamic_slice_in_dim(x, index * rows, rows)
    sent = [lax.dynamic_slice_in_dim(x, (index ^ mask) * rows, rows).astype(BF16) for mask in range(1, size)]
    parts = [swap(out, axes, mask) for mask, out in enumerate(sent, 1)]
    for part in parts:
        total = total + part.astype(F32)
    return total


def full_sum(x, axes):
    groups = [axes] if size_of(axes) <= 4 else [(a,) for a in axes]
    for group in groups:
        size = size_of(group)
        sent = x.astype(BF16)
        parts = [sent] + [swap(sent, group, mask) for mask in range(1, size)]
        span = size
        while span > 1:
            parts = [parts[i].astype(F32) + parts[i + span // 2].astype(F32) for i in range(span // 2)]
            span //= 2
        x = parts[0]
    return x


def gather_rows(x, axes):
    size = size_of(axes)
    if size == 1:
        return x
    index = lax.axis_index(axes)
    full = jnp.zeros((size * x.shape[0],) + x.shape[1:], x.dtype)
    full = lax.dynamic_update_slice_in_dim(full, x, index * x.shape[0], 0)
    for mask in range(1, size):
        part = swap(x, axes, mask)
        full = lax.dynamic_update_slice_in_dim(full, part, (index ^ mask) * x.shape[0], 0)
    return full


def on_device(pooled, proj, centers, labels, row_weight):
    s_axes = ("sz", "sy")
    ns, nk, nl = size_of(s_axes), size_of(("k",)), size_of(("dl",))
    rows, _ = pooled.shape
    c_dev = centers.shape[0]
    half = c_dev // nl
    at_s, at_k, at_l = (lax.axis_index(a) for a in (s_axes, "k", "dl"))
    split = lax.optimization_barrier(
        tuple(lax.dynamic_slice_in_dim(centers, (at_l ^ c) * half, half) for c in range(nl))
    )
    own_parts = [split[0]] + [swap(split[0], ("k",), j) for j in range(1, nk)]
    blocks = [pooled] + [swap(pooled, s_axes, m) for m in range(1, ns)]
    meta = lax.optimization_barrier(jnp.concatenate([labels.astype(F32), row_weight.astype(F32)]).reshape(1, 2 * rows))
    metas = [meta] + [swap(meta, s_axes, m) for m in range(1, ns)]
    cents = list(own_parts)
    for c in range(1, nl):
        cents.append(split[c])
        cents += [swap(own_parts[j], ("dl",), c) for j in range(1, nk)]
    pairs = [unit_rows(part.astype(F32)) for part in cents]
    unit = jnp.concatenate([p[0] for p in pairs], axis=0)
    c_inv = pairs[0][1]
    label_all = jnp.concatenate([m[:, :rows] for m in metas], axis=1).astype(jnp.int32)
    weight_all = jnp.concatenate([m[:, rows:] for m in metas], axis=1)
    local = lax.broadcasted_iota(jnp.int32, (half, 1), 0)
    ids = jnp.concatenate(
        [local + ((at_k ^ j) * ns + at_s) * c_dev + (at_l ^ c) * half for c in range(nl) for j in range(nk)], axis=0
    )
    feats = jnp.concatenate(blocks, axis=0)
    emb, z_inv = unit_rows(dot(feats, proj, 1, 0))
    onehot = (ids == label_all).astype(F32)
    logits = SCALE * dot(unit, emb, 1, 1) - SCALE * MARGIN * onehot
    expo = jnp.exp(logits)
    stats = jnp.concatenate(
        [jnp.sum(expo, axis=0, keepdims=True), jnp.sum(logits * onehot, axis=0, keepdims=True)], axis=1
    )
    total, target = stats[:, : ns * rows], stats[:, ns * rows : ns * rows + rows]
    for m in range(1, ns):
        other = swap(stats, s_axes, m)
        total = total + jnp.concatenate([other[:, (b ^ m) * rows : ((b ^ m) + 1) * rows] for b in range(ns)], axis=1)
        target = target + other[:, (ns + m) * rows : (ns + m + 1) * rows]
    row_loss = (jnp.log(total[:, :rows]) - target).reshape(rows)
    grad = (weight_all * (expo / total - onehot)).astype(BF16)
    grad_emb = SCALE * dot(grad, unit, 0, 0)
    emb_f = emb.astype(F32)
    grad_hidden = (z_inv * (grad_emb - emb_f * jnp.sum(emb_f * grad_emb, axis=1, keepdims=True))).astype(BF16)

    span = nk * half
    own = SCALE * dot(grad[:span], emb, 1, 0)
    for c in range(1, nl):
        send = (SCALE * dot(grad[c * span : (c + 1) * span], emb, 1, 0)).astype(BF16)
        own = own + swap(send, ("dl",), c).astype(F32)
    summed = own[:half]
    for j in range(1, nk):
        summed = summed + swap(own[j * half : (j + 1) * half].astype(BF16), ("k",), j).astype(F32)
    summed = full_sum(summed, ("dh",))
    unit_f = unit[:half].astype(F32)
    center_part = c_inv * (summed - unit_f * jnp.sum(unit_f * summed, axis=1, keepdims=True))
    center_grad = gather_rows(center_part, ("dl",))
    first, second = ("dh", "sy"), ("k", "sz")
    cols = feats.shape[1] // nl
    sends = [dot(lax.dynamic_slice_in_dim(feats, (at_l ^ c) * cols, cols, 1), grad_hidden, 0, 0).astype(BF16) for c in range(1, nl)]
    piece = dot(lax.dynamic_slice_in_dim(feats, at_l * cols, cols, 1), grad_hidden, 0, 0)
    piece = lax.optimization_barrier(piece)
    for c in range(1, nl):
        piece = piece + swap(sends[c - 1], ("dl",), c).astype(F32)
    piece = scatter_sum(piece, first)
    piece = full_sum(piece, second)
    piece = piece.astype(BF16)
    mine = gather_rows(piece, first)
    others = [swap(mine, ("dl",), c) for c in range(1, nl)]
    proj_grad = lax.optimization_barrier(jnp.concatenate([mine] * nl, axis=0).astype(F32))
    for c, other in enumerate(others, 1):
        proj_grad = lax.dynamic_update_slice_in_dim(proj_grad, other.astype(F32), (at_l ^ c) * cols, 0)
    return (row_loss, center_grad, proj_grad)


def solution(mesh):
    dp, cls = mesh.shape["dp"], mesh.shape["cls"]
    nl = 2 if dp % 2 == 0 else 1
    bits = cls.bit_length() - 1
    ns = 1 << ((bits + 1) // 2)
    sy = min(2, ns)
    fine = jax.sharding.Mesh(
        mesh.devices.reshape(dp // nl, nl, cls // ns, ns // sy, sy), ("dh", "dl", "k", "sz", "sy")
    )
    dp_axes, cls_axes = ("dh", "dl"), ("k", "sz", "sy")
    every = dp_axes + cls_axes
    in_specs = (P(every, None), P(), P(cls_axes, None), P(every), P(every))
    out_specs = (P(every), P(cls_axes, None), P())

    return jax.shard_map(on_device, mesh=fine, in_specs=in_specs, out_specs=out_specs, check_vma=False)
```
